32 devices in a mesh: wide: 8 (over z, x), narrow: 4 (over y, core).
Axes of the slice: x: 2, y: 2, z: 4, core: 2. Of those that a mesh axis runs over, the one named last changes fastest.
Arguments:
- words_first: bfloat16 [32, 512, 768], P(('wide', 'narrow')), may hold values from -6 to 6
- entities_first: bfloat16 [32, 128, 768], P(('wide', 'narrow')), may hold values from -6 to 6
- positions_first: int32 [32, 128], P(('wide', 'narrow')), may hold values from 0 to 511
- entity_slots_first: int32 [32, 12], P(('wide', 'narrow')), may hold values from -1 to 127, as said below
- entity_labels_first: int32 [32, 12], P(('wide', 'narrow')), may hold values from 0 to 32767
- words_second: bfloat16 [32, 512, 768], P(('wide', 'narrow')), may hold values from -6 to 6
- entities_second: bfloat16 [32, 128, 768], P(('wide', 'narrow')), may hold values from -6 to 6
- positions_second: int32 [32, 128], P(('wide', 'narrow')), may hold values from 0 to 511
- word_slots_second: int32 [32, 64], P(('wide', 'narrow')), may hold values from -1 to 511, as said below
- word_labels_second: int32 [32, 64], P(('wide', 'narrow')), may hold values from 0 to 4095
- entity_slots_second: int32 [32, 12], P(('wide', 'narrow')), may hold values from -1 to 127, as said below
- entity_labels_second: int32 [32, 12], P(('wide', 'narrow')), may hold values from 0 to 32767
- query_word_word: bfloat16 [768, 768], P('narrow'), may hold values from -0.21875 to 0.21875
- query_word_entity: bfloat16 [768, 768], P('narrow'), may hold values from -0.21875 to 0.21875
- query_entity_word: bfloat16 [768, 768], P('narrow'), may hold values from -0.21875 to 0.21875
- query_entity_entity: bfloat16 [768, 768], P('narrow'), may hold values from -0.21875 to 0.21875
- key_weight: bfloat16 [768, 768], P('narrow'), may hold values from -0.21875 to 0.21875
- value_weight: bfloat16 [768, 768], P('narrow'), may hold values from -0.21875 to 0.21875
- output_weight: bfloat16 [768, 768], P('narrow'), may hold values from -3 to 3
- attention_gain: bfloat16 [768], P('narrow'), may hold values from 0.5 to 1.5
- attention_bias: bfloat16 [768], P('narrow'), may hold values from -2 to 2
- up_weight: bfloat16 [768, 3072], P('narrow'), may hold values from -0.21875 to 0.21875
- down_weight: bfloat16 [3072, 768], P('narrow'), may hold values from -0.109375 to 0.109375
- feedforward_gain: bfloat16 [768], P('narrow'), may hold values from 0.5 to 1.5
- feedforward_bias: bfloat16 [768], P('narrow'), may hold values from -2 to 2
- word_table: bfloat16 [4096, 768], P(('wide', 'narrow')), may hold values from -0.4375 to 0.4375
- entity_dense: bfloat16 [768, 256], P('narrow'), may hold values from -0.21875 to 0.21875
- entity_table: bfloat16 [32768, 256], P(('wide', 'narrow')), may hold values from -1 to 1
- position_table: bfloat16 [512, 768], P('narrow'), may hold values from -3 to 3
Outputs:
- entity_word_grad_first: float32 [768, 768], P('narrow')
- entity_entity_grad_first: float32 [768, 768], P('narrow')
- loss_second: float32 [], replicated
- words_grad: bfloat16 [32, 512, 768], P(('wide', 'narrow'))
- entities_grad: bfloat16 [32, 128, 768], P(('wide', 'narrow'))
- query_word_word_grad: float32 [768, 768], P('narrow')
- query_word_entity_grad: float32 [768, 768], P('narrow')
- query_entity_word_grad: float32 [768, 768], P('narrow')
- query_entity_entity_grad: float32 [768, 768], P('narrow')
- key_weight_grad: float32 [768, 768], P('narrow')
- value_weight_grad: float32 [768, 768], P('narrow')
- output_weight_grad: float32 [768, 768], P('narrow')
- attention_gain_grad: float32 [768], P('narrow')
- attention_bias_grad: float32 [768], P('narrow')
- up_weight_grad: float32 [768, 3072], P('narrow')
- down_weight_grad: float32 [3072, 768], P('narrow')
- feedforward_gain_grad: float32 [768], P('narrow')
- feedforward_bias_grad: float32 [768], P('narrow')
- word_table_grad: float32 [4096, 768], P(('wide', 'narrow'))
- entity_dense_grad: float32 [768, 256], P('narrow')
- entity_table_grad: float32 [32768, 256], P(('wide', 'narrow'))
- position_table_grad: float32 [512, 768], P('narrow')
The draws below stay inside these ranges and needn't reach their ends.
Inputs may be any that keep to these rules, and one draw needn't show every extreme that they name: `word_slots_second`: in each row the used slots come first and hold distinct word positions, the rest hold -1; some row of the batch uses all 64 slots. `entity_slots_first`: in each row the used slots come first and hold distinct entity positions, the rest hold -1; some row of the batch uses all 12 slots. `entity_slots_second`: in each row the used slots come first and hold distinct entity positions, the rest hold -1; some row of the batch uses all 12 slots.
All inputs are finite; a program needn't handle non-finite values.
Results may differ from the reference program's by a relative error of at most 0.025.
The reference program's roundings to bfloat16 on the way count: a program that leaves them out, or rounds other values in their place, can miss the bound.
Values may be sent and summed in bfloat16 or wider, within the bound.
No kernel may reach another device: no remote copies, remote signals or barrier semaphores. Data moves between devices by JAX's collectives and lax.ppermute only.
A program may use at most 576 MiB of HBM per device.

```python
import math
import jax
import jax.numpy as jnp
import numpy as np
from jax import lax

D = 768
HEADS = 12
HD = 64
FF = 3072
ENT_DIM = 256
WORDS = 512
ENTS = 128
SW = 64
SE = 12
ROWS = 32
VOCAB = 4096
ENT_VOCAB = 32768


def slot_table(key, row_count, slot_width, position_count):
    order_key, count_key = jax.random.split(key)
    scores = jax.random.randint(order_key, (row_count, position_count), 0, 1 << 20) * position_count
    scores = scores + jnp.arange(position_count, dtype=jnp.int32)[None, :]
    order = jnp.argsort(scores, axis=1).astype(jnp.int32)
    picked = order[:, :slot_width]
    row_number = jnp.arange(row_count, dtype=jnp.int32)
    lowest = slot_width // 3
    ramp = (slot_width - lowest) * row_number // max(row_count - 1, 1)
    jitter = jax.random.randint(count_key, (row_count,), -2, 3)
    used = jnp.clip(lowest + ramp + jitter, 1, slot_width)
    used = jnp.where(row_number == row_count - 1, slot_width, used)
    column = jnp.arange(slot_width, dtype=jnp.int32)[None, :]
    return jnp.where(column < used[:, None], picked, -1).astype(jnp.int32)


def draw_entity_slots_first(key, part):
    return slot_table(jax.random.fold_in(key, 11), ROWS, SE, ENTS)


def draw_word_slots_second(key, part):
    return slot_table(jax.random.fold_in(key, 23), ROWS, SW, WORDS)


def draw_entity_slots_second(key, part):
    return slot_table(jax.random.fold_in(key, 37), ROWS, SE, ENTS)


def place_ends(drawn, rng, low, top_value):
    longest = drawn.shape.index(max(drawn.shape))
    spots = []
    for shift in (0, 1):
        where = [jax.random.randint(jax.random.fold_in(rng, axis), (), 0, length) for axis, length in enumerate(drawn.shape)]
        where[longest] = (where[longest] + shift) % drawn.shape[longest]
        spots.append(tuple(where))
    return drawn.at[spots[0]].set(low).at[spots[1]].set(top_value)


def block_scale(stream_key, dims, pieces, smallest, largest):
    def one(dim, shards_of):
        draws = jax.random.uniform(jax.random.fold_in(jax.random.fold_in(stream_key, 6), dim), (shards_of,), jnp.float32, smallest / len(pieces), largest / len(pieces))
        return jnp.repeat(jnp.exp(draws), dims[dim] // shards_of).reshape((-1,) + (1,) * (len(dims) - dim - 1))

    loudness = one(*pieces[0])
    for cut in pieces[1:]:
        loudness = loudness * one(*cut)
    return loudness


def cumulative_ranks(count, skew):
    weights = [(1 << 20) // math.isqrt(grade ** skew) + 1 for grade in range(1, count + 1)]
    scale = 1 + sum(weights) // (1 << 30)
    return np.cumsum(np.array([max(1, weight // scale) for weight in weights]))


def ranked_ids(own_key, dims, amount, lean):
    listing = cumulative_ranks(amount, lean)
    lot = jax.random.randint(jax.random.fold_in(own_key, 1), dims, 0, int(listing[amount - 1]))
    grade = jnp.searchsorted(jnp.asarray(listing, jnp.int32), lot, side="right")
    return jax.random.permutation(jax.random.fold_in(own_key, 2), amount)[grade].astype(jnp.int32)


def scatter_about(stream_key, extent, width, bound, cuts=(), held_as=jnp.bfloat16):
    result = jax.random.normal(stream_key, extent, jnp.float32) * width
    if len(cuts) > 0:
        result = block_scale(stream_key, extent, cuts, -0.22, 0.18) * result
    return jnp.clip(result, min=-bound, max=bound).astype(held_as)


def setup_inputs(seed: int = 0) -> dict:
    streams_of = jax.random.split(jax.random.key(seed), 30)
    return {
        "words_first": scatter_about(streams_of[0], (ROWS, WORDS, D), 1.0, 6.0, ((0, 32),)),
        "entities_first": scatter_about(streams_of[1], (ROWS, ENTS, D), 1.0, 6.0, ((0, 32),)),
        "positions_first": place_ends(jax.random.randint(streams_of[2], (ROWS, ENTS), 0, WORDS), jax.random.fold_in(streams_of[2], 1), 0, WORDS - 1).astype(jnp.int32),
        "entity_slots_first": draw_entity_slots_first(jax.random.fold_in(streams_of[29], 71), 0),
        "entity_labels_first": place_ends(jax.random.randint(streams_of[4], (ROWS, SE), 0, ENT_VOCAB), jax.random.fold_in(streams_of[4], 1), 0, ENT_VOCAB - 1).astype(jnp.int32),
        "words_second": scatter_about(streams_of[5], (ROWS, WORDS, D), 1.0, 6.0, ((0, 32),)),
        "entities_second": scatter_about(streams_of[6], (ROWS, ENTS, D), 1.0, 6.0, ((0, 32),)),
        "positions_second": place_ends(jax.random.randint(streams_of[7], (ROWS, ENTS), 0, WORDS), jax.random.fold_in(streams_of[7], 1), 0, WORDS - 1).astype(jnp.int32),
        "word_slots_second": draw_word_slots_second(jax.random.fold_in(streams_of[29], 71), 0),
        "word_labels_second": place_ends(ranked_ids(streams_of[9], (ROWS, SW), VOCAB, 2), jax.random.fold_in(streams_of[9], 3), 0, VOCAB - 1).astype(jnp.int32),
        "entity_slots_second": draw_entity_slots_second(jax.random.fold_in(streams_of[29], 71), 0),
        "entity_labels_second": place_ends(jax.random.randint(streams_of[11], (ROWS, SE), 0, ENT_VOCAB), jax.random.fold_in(streams_of[11], 1), 0, ENT_VOCAB - 1).astype(jnp.int32),
        "query_word_word": scatter_about(streams_of[12], (D, D), D ** -0.5, 0.21875, ((0, 4),)),
        "query_word_entity": scatter_about(streams_of[13], (D, D), D ** -0.5, 0.21875, ((0, 4),)),
        "query_entity_word": scatter_about(streams_of[14], (D, D), D ** -0.5, 0.21875, ((0, 4),)),
        "query_entity_entity": scatter_about(streams_of[15], (D, D), D ** -0.5, 0.21875, ((0, 4),)),
        "key_weight": scatter_about(streams_of[16], (D, D), D ** -0.5, 0.21875, ((0, 4),)),
        "value_weight": scatter_about(streams_of[17], (D, D), D ** -0.5, 0.21875, ((0, 4),)),
        "output_weight": scatter_about(streams_of[18], (D, D), (max(D // 192, 1)) ** -0.5, 3.0, ((0, 4),)),
        "attention_gain": jnp.clip(1.0 + 0.1 * jax.random.normal(streams_of[19], (D,), jnp.float32), 0.5, 1.5).astype(jnp.bfloat16),
        "attention_bias": scatter_about(streams_of[20], (D,), 0.3, 2.0, ((0, 4),)),
        "up_weight": scatter_about(streams_of[21], (D, FF), D ** -0.5, 0.21875, ((0, 4),)),
        "down_weight": scatter_about(streams_of[22], (FF, D), FF ** -0.5, 0.109375, ((0, 4),)),
        "feedforward_gain": jnp.clip(1.0 + 0.1 * jax.random.normal(streams_of[23], (D,), jnp.float32), 0.5, 1.5).astype(jnp.bfloat16),
        "feedforward_bias": scatter_about(streams_of[24], (D,), 0.3, 2.0, ((0, 4),)),
        "word_table": scatter_about(streams_of[25], (VOCAB, D), (D // 4) ** -0.5, 0.4375, ((0, 32),)),
        "entity_dense": scatter_about(streams_of[26], (D, ENT_DIM), D ** -0.5, 0.21875, ((0, 4),)),
        "entity_table": scatter_about(streams_of[27], (ENT_VOCAB, ENT_DIM), (max(ENT_DIM // 9, 1)) ** -0.5, 1.0, ((0, 32),)),
        "position_table": scatter_about(streams_of[28], (WORDS, D), 0.5, 3.0, ((0, 4),)),
    }


EPS = 1e-05

@jax.custom_vjp
def low(v):
    return lax.optimization_barrier(v.astype(jnp.bfloat16)).astype(jnp.float32)

@jax.custom_vjp
def low_back(v):
    return v

def low_keep(v):
    return (low(v), None)

def low_pass(kept, grad):
    return (grad,)

def back_keep(v):
    return (v, None)

def back_low(kept, grad):
    return (low(grad),)
low.defvjp(low_keep, low_pass)
low_back.defvjp(back_keep, back_low)

def rounded(value):
    return low(low_back(value))

def project(inputs, weight):
    return jnp.einsum('gld,de->gle', inputs, weight, precision=lax.Precision.HIGHEST)

def gather_rows(values, position):
    return jax.vmap(lambda table, picked: table[picked])(values, position)

def layer_norm(resid, gain, bias):
    average = lax.optimization_barrier(jnp.mean(resid, axis=-1, keepdims=True))
    centered = resid - average
    spread = lax.optimization_barrier(jnp.mean(centered * centered, axis=-1, keepdims=True))
    return centered * lax.rsqrt(spread + EPS) * gain + bias

def head_loss(logits, labels, valid):
    top = lax.optimization_barrier(jnp.max(logits, axis=-1, keepdims=True))
    total = top[..., 0] + jnp.log(lax.optimization_barrier(jnp.sum(jnp.exp(logits - top), axis=-1)))
    chosen = jnp.take_along_axis(logits, labels[..., None], axis=-1)[..., 0]
    return jnp.sum((total - chosen) * valid)

def block_loss(weights, words, entities, positions, entity_slots, entity_labels, entity_scale, word_part):
    query_word_word, query_word_entity, query_entity_word, query_entity_entity, key_weight, value_weight, output_weight, attention_gain, attention_bias, up_weight, down_weight, feedforward_gain, feedforward_bias, word_table, entity_dense, entity_table, position_table = weights
    split = WORDS
    group = words.shape[0]
    length = WORDS + ENTS
    tokens = jnp.concatenate([words, entities + position_table[positions]], axis=1)
    tokens_low = low(tokens)
    word_low = tokens_low[:, :split]
    entity_low = tokens_low[:, split:]
    first_q = jnp.concatenate([rounded(project(word_low, query_word_word)), rounded(project(entity_low, query_entity_word))], axis=1)
    second_q = jnp.concatenate([rounded(project(word_low, query_word_entity)), rounded(project(entity_low, query_entity_entity))], axis=1)
    keys = rounded(project(tokens_low, key_weight))
    values = rounded(project(tokens_low, value_weight))

    def split_heads(array):
        return array.reshape(group, length, HEADS, HD)
    first_heads = split_heads(first_q)
    second_heads = split_heads(second_q)
    key_heads = split_heads(keys)
    value_heads = split_heads(values)
    scores = jnp.concatenate([jnp.einsum('gqhd,gkhd->ghqk', first_heads, key_heads[:, :split], precision=lax.Precision.HIGHEST), jnp.einsum('gqhd,gkhd->ghqk', second_heads, key_heads[:, split:], precision=lax.Precision.HIGHEST)], axis=-1)
    scores = low_back(scores * HD ** (-0.5))
    top = lax.optimization_barrier(jnp.max(scores, axis=-1, keepdims=True))
    expo = jnp.exp(scores - top)
    probs = expo / lax.optimization_barrier(jnp.sum(expo, axis=-1, keepdims=True))
    context = jnp.einsum('ghqk,gkhd->gqhd', low(probs), value_heads, precision=lax.Precision.HIGHEST)
    context = rounded(context.reshape(group, length, HEADS * HD))
    resid_one = tokens + low_back(project(context, output_weight))
    hidden_one = layer_norm(resid_one, attention_gain, attention_bias)
    up = low_back(project(low(hidden_one), up_weight))
    act = low(jax.nn.gelu(up, approximate=False))
    hidden_two = layer_norm(hidden_one + low_back(project(act, down_weight)), feedforward_gain, feedforward_bias)
    entity_valid = (entity_slots >= 0).astype(jnp.float32)
    picked = low(gather_rows(hidden_two[:, split:], jnp.maximum(entity_slots, 0)))
    mapped = rounded(jnp.einsum('gsd,de->gse', picked, entity_dense, precision=lax.Precision.HIGHEST))
    entity_logits = low_back(jnp.einsum('gse,ve->gsv', mapped, entity_table, precision=lax.Precision.HIGHEST))
    loss = head_loss(entity_logits, entity_labels, entity_valid) * entity_scale
    if word_part is not None:
        word_slots, word_labels, word_scale = word_part
        word_rows = low(gather_rows(hidden_two[:, :split], jnp.maximum(word_slots, 0)))
        word_logits = low_back(jnp.einsum('gsd,vd->gsv', word_rows, word_table, precision=lax.Precision.HIGHEST))
        loss = loss + head_loss(word_logits, word_labels, (word_slots >= 0).astype(jnp.float32)) * word_scale
    return loss

def run_phase(weights, words, entities, positions, entity_slots, entity_labels, entity_scale, word_slots, word_labels, word_scale):
    group = 4 if ROWS % 4 == 0 else 1
    with_words = word_slots is not None
    stacked = [words, entities, positions, entity_slots, entity_labels]
    if with_words:
        stacked = stacked + [word_slots, word_labels]
    blocks = tuple((array.reshape((ROWS // group, group) + array.shape[1:]) for array in stacked))

    def step(carry, block):
        grads, running = carry
        word_part = (block[5], block[6], word_scale) if with_words else None

        def closed(params, block_words, block_entities):
            return block_loss(params, block_words, block_entities, block[2], block[3], block[4], entity_scale, word_part)
        loss, pull = jax.vjp(closed, weights, block[0].astype(jnp.float32), block[1].astype(jnp.float32))
        param_grads, words_grad, entities_grad = pull(jnp.ones_like(loss))
        grads = tuple((earlier + update for earlier, update in zip(grads, param_grads)))
        return ((grads, running + loss), (words_grad, entities_grad))
    start = (tuple((jnp.zeros_like(weight) for weight in weights)), jnp.zeros((), jnp.float32))
    (grads, running), (words_grad, entities_grad) = lax.scan(step, start, blocks)
    return (grads, running, words_grad.reshape(words.shape), entities_grad.reshape(entities.shape))

def reference(words_first, entities_first, positions_first, entity_slots_first, entity_labels_first, words_second, entities_second, positions_second, word_slots_second, word_labels_second, entity_slots_second, entity_labels_second, query_word_word, query_word_entity, query_entity_word, query_entity_entity, key_weight, value_weight, output_weight, attention_gain, attention_bias, up_weight, down_weight, feedforward_gain, feedforward_bias, word_table, entity_dense, entity_table, position_table):
    weights = tuple((weight.astype(jnp.float32) for weight in (query_word_word, query_word_entity, query_entity_word, query_entity_entity, key_weight, value_weight, output_weight, attention_gain, attention_bias, up_weight, down_weight, feedforward_gain, feedforward_bias, word_table, entity_dense, entity_table, position_table)))
    count_entity_one = jnp.sum(entity_slots_first >= 0).astype(jnp.float32)
    count_word_two = jnp.sum(word_slots_second >= 0).astype(jnp.float32)
    count_entity_two = jnp.sum(entity_slots_second >= 0).astype(jnp.float32)
    grads_one, loss_one, unused_words, unused_entities = run_phase(weights, words_first, entities_first, positions_first, entity_slots_first, entity_labels_first, 1.0 / count_entity_one, None, None, None)
    grads_two, loss_two, words_grad, entities_grad = run_phase(weights, words_second, entities_second, positions_second, entity_slots_second, entity_labels_second, 1.0 / count_entity_two, word_slots_second, word_labels_second, 1.0 / count_word_two)
    return (grads_one[2], grads_one[3], loss_two, words_grad.astype(jnp.bfloat16), entities_grad.astype(jnp.bfloat16), grads_two[0], grads_two[1], grads_two[2], grads_two[3], grads_two[4], grads_two[5], grads_two[6], grads_two[7], grads_two[8], grads_two[9], grads_two[10], grads_two[11], grads_two[12], grads_two[13], grads_two[14], grads_two[15], grads_two[16])
```

```python
import jax
import jax.numpy as jnp
from jax import lax
from jax.sharding import PartitionSpec as P

HEADS = 12
HD = 64


EPS = 1e-05
HALF_ROOT = 0.7071067811865476
NORMAL_PEAK = 0.3989422804014327

WIDTH = 768
PAD = 16


def bits_of(axis):
    size = lax.axis_size(axis)
    masks = []
    mask = 1
    while mask < size:
        masks.append(mask)
        mask *= 2
    return masks


def exchange(value, axis, mask):
    size = lax.axis_size(axis)
    return lax.ppermute(value, axis, [(place, place ^ mask) for place in range(size)])


def joined_low(mine, theirs):
    return (mine.astype(jnp.float32) + theirs.astype(jnp.float32)).astype(jnp.bfloat16)


def mesh_stages():
    wide = [("wide", mask) for mask in reversed(bits_of("wide"))]
    return wide + [("narrow", mask) for mask in reversed(bits_of("narrow"))]


def relative_ids():
    ids = [0]
    for axis, mask in mesh_stages():
        step = mask * (lax.axis_size("narrow") if axis == "wide" else 1)
        ids = ids + [one ^ step for one in ids]
    return ids


def gather_relative(block):
    value = block[None]
    for axis, mask in mesh_stages():
        value = jnp.concatenate([value, exchange(value, axis, mask)], axis=0)
    return value


def scatter_relative(value):
    for axis, mask in reversed(mesh_stages()):
        half = value.shape[0] // 2
        value = joined_low(value[:half], exchange(value[half:], axis, mask))
    return value[0]


def flipped(value, stage):
    shaped = value.reshape((-1, 2, 1 << stage) + value.shape[1:])
    return jnp.concatenate([shaped[:, 1:], shaped[:, :1]], axis=1).reshape(value.shape)


def join_norms(norms):
    for stage, (axis, mask) in enumerate(mesh_stages()):
        theirs = exchange(flipped(norms, stage), axis, mask)
        top = jnp.maximum(norms, theirs)
        norms = top + jnp.log(jnp.exp(norms - top) + jnp.exp(theirs - top))
    return norms


def halves(value, axis, mask):
    side = (lax.axis_index(axis) // mask) % 2
    mine = lax.dynamic_index_in_dim(value, side, 1, keepdims=False)
    theirs = lax.dynamic_index_in_dim(value, 1 - side, 1, keepdims=False)
    return (mine, theirs)


def reduce_chunk(blocks):
    value = blocks
    rows = blocks.shape[1]
    for mask in bits_of("narrow"):
        mine, theirs = halves(value.reshape(value.shape[0] // 2, 2, rows, WIDTH), "narrow", mask)
        value = joined_low(mine, exchange(theirs, "narrow", mask))
    value = value[0]
    for mask in bits_of("wide"):
        mine, theirs = halves(value.reshape(1, 2, value.shape[0] // 2, WIDTH), "wide", mask)
        value = joined_low(mine[0], exchange(theirs[0], "wide", mask))
    for mask in reversed(bits_of("wide")):
        side = (lax.axis_index("wide") // mask) % 2
        theirs = exchange(value, "wide", mask)
        value = jnp.where(
            side == 0,
            jnp.concatenate([value, theirs], axis=0),
            jnp.concatenate([theirs, value], axis=0),
        )
    return value


def narrow_blocks(grad):
    count = lax.axis_size("narrow")
    grad = grad.astype(jnp.bfloat16)
    rows, columns = grad.shape
    if columns <= WIDTH:
        return grad.reshape(count, rows // count * columns // WIDTH, WIDTH)
    pieces = [
        grad[:, start : start + WIDTH].reshape(count, rows // count, WIDTH)
        for start in range(0, columns, WIDTH)
    ]
    return jnp.concatenate(pieces, axis=1)


def whole_shard(rows, shape):
    if shape[1] <= WIDTH:
        return rows.reshape(shape)
    pieces = jnp.split(rows, shape[1] // WIDTH, axis=0)
    return jnp.concatenate(pieces, axis=1)


def padded_rows(value, multiple):
    extra = -value.shape[-2] % multiple
    pads = [(0, 0)] * (value.ndim - 2) + [(0, extra), (0, 0)]
    return jnp.pad(value, pads) if extra else value


def reduce_grads(grads):
    count = lax.axis_size("narrow")
    blocks = [narrow_blocks(grad) for grad in grads]
    packed = padded_rows(jnp.concatenate(blocks, axis=1), PAD * lax.axis_size("wide"))
    total = reduce_chunk(packed)
    shards = []
    start = 0
    for grad, block in zip(grads, blocks):
        stop = start + block.shape[1]
        shape = (grad.shape[0] // count, grad.shape[1])
        shards.append(whole_shard(total[start:stop], shape).astype(jnp.float32))
        start = stop
    return shards


def gather_weights(shards):
    pieces = []
    for shard in shards:
        if shard.ndim == 1:
            pieces.append(jnp.pad(shard, (0, WIDTH - shard.shape[0]))[None])
        elif shard.shape[1] <= WIDTH:
            pieces.append(shard.reshape(-1, WIDTH))
        else:
            pieces += jnp.split(shard, shard.shape[1] // WIDTH, axis=1)
    packed = padded_rows(jnp.concatenate(pieces, axis=0), PAD)
    full = lax.all_gather(packed, "narrow")
    count = full.shape[0]
    whole = []
    start = 0
    for shard in shards:
        if shard.ndim == 1:
            whole.append(full[:, start, : shard.shape[0]].reshape(-1))
            start += 1
        elif shard.shape[1] <= WIDTH:
            rows = shard.shape[0] * shard.shape[1] // WIDTH
            whole.append(full[:, start : start + rows].reshape(-1, shard.shape[1]))
            start += rows
        else:
            rows = shard.shape[0]
            blocks = []
            for _ in range(shard.shape[1] // WIDTH):
                blocks.append(full[:, start : start + rows].reshape(count * rows, WIDTH))
                start += rows
            whole.append(jnp.concatenate(blocks, axis=1))
    return whole


def as_digits(tags):
    raised = tags + 1
    digits = jnp.stack([raised % 256, raised // 256 % 256, raised // 65536])
    return digits.astype(jnp.bfloat16)


def from_digits(digits):
    whole = digits.astype(jnp.int32)
    return whole[..., 0, :] + 256 * whole[..., 1, :] + 65536 * whole[..., 2, :] - 1


def matmul(inputs, weight):
    return jnp.einsum("rld,de->rle", inputs, weight, preferred_element_type=jnp.float32)


def matmul_back(grads, weight):
    return jnp.einsum("rle,de->rld", grads, weight, preferred_element_type=jnp.float32)


def weight_grad(inputs, grads):
    return jnp.einsum("rld,rle->de", inputs, grads, preferred_element_type=jnp.float32)


def gather_rows(values, position):
    return jax.vmap(lambda table, picked: table[picked])(values, position)


def spread_rows(grads, position, length):
    onehot = (position[:, :, None] == jnp.arange(length)[None, None, :]).astype(jnp.float32)
    return jnp.einsum("rsn,rsd->rnd", onehot, grads, precision=lax.Precision.HIGHEST)


def head_groups():
    return 2


def to_groups(values):
    rows, count = (values.shape[0], values.shape[1])
    groups = head_groups()
    shaped = values.reshape(rows, count, groups, HEADS // groups, HD)
    return jnp.transpose(shaped, (0, 2, 1, 3, 4)).reshape(rows * groups, count, HEADS // groups, HD)


def from_groups(values, rows):
    groups = head_groups()
    count = values.shape[1]
    shaped = values.reshape(rows, groups, count, HEADS // groups, HD)
    return jnp.transpose(shaped, (0, 2, 1, 3, 4)).reshape(rows, count, HEADS * HD)


def norm_forward(resid, gain, bias):
    average = jnp.mean(resid, axis=-1, keepdims=True)
    centered = resid - average
    inverse = lax.rsqrt(jnp.mean(centered * centered, axis=-1, keepdims=True) + EPS)
    normal = centered * inverse
    return (normal * gain.astype(jnp.float32) + bias.astype(jnp.float32), normal, inverse)


def norm_backward(grads, normal, inverse, gain):
    scaled = grads * gain.astype(jnp.float32)
    centered = scaled - jnp.mean(scaled, axis=-1, keepdims=True)
    resid_grad = inverse * (centered - normal * jnp.mean(scaled * normal, axis=-1, keepdims=True))
    return (resid_grad, jnp.sum(grads * normal, axis=(0, 1)), jnp.sum(grads, axis=(0, 1)))


def score_block(first, second, keys, split):
    scores = jnp.concatenate(
        [
            jnp.einsum("qhd,khd->hqk", first, keys[:split], preferred_element_type=jnp.float32),
            jnp.einsum("qhd,khd->hqk", second, keys[split:], preferred_element_type=jnp.float32),
        ],
        axis=-1,
    )
    return scores * HD ** (-0.5)


def attention_forward(first, second, keys, values, split):
    scores = score_block(first, second, keys, split)
    top = jnp.max(scores, axis=-1, keepdims=True)
    expo = jnp.exp(scores - top)
    total = jnp.sum(expo, axis=-1, keepdims=True)
    probs_low = (expo / total).astype(jnp.bfloat16)
    context = jnp.einsum("hqk,khd->qhd", probs_low, values, preferred_element_type=jnp.float32)
    return (context.astype(jnp.bfloat16), (top + jnp.log(total))[..., 0])


def attention_backward(first, second, keys, values, lse, context_grad, split, with_keys):
    scale = HD ** (-0.5)
    scores = score_block(first, second, keys, split)
    probs = jnp.exp(scores - lse[..., None])
    probs_grad = jnp.einsum(
        "qhd,khd->hqk", context_grad, values, preferred_element_type=jnp.float32
    )
    scores_grad = (
        probs * (probs_grad - jnp.sum(probs * probs_grad, axis=-1, keepdims=True))
    ).astype(jnp.bfloat16)
    first_grad = (
        jnp.einsum(
            "hqk,khd->qhd",
            scores_grad[..., :split],
            keys[:split],
            preferred_element_type=jnp.float32,
        )
        * scale
    )
    second_grad = (
        jnp.einsum(
            "hqk,khd->qhd",
            scores_grad[..., split:],
            keys[split:],
            preferred_element_type=jnp.float32,
        )
        * scale
    )
    if not with_keys:
        return (first_grad, second_grad)
    keys_grad = (
        jnp.concatenate(
            [
                jnp.einsum(
                    "hqk,qhd->khd",
                    scores_grad[..., :split],
                    first,
                    preferred_element_type=jnp.float32,
                ),
                jnp.einsum(
                    "hqk,qhd->khd",
                    scores_grad[..., split:],
                    second,
                    preferred_element_type=jnp.float32,
                ),
            ],
            axis=0,
        )
        * scale
    )
    values_grad = jnp.einsum(
        "hqk,qhd->khd", probs.astype(jnp.bfloat16), context_grad, preferred_element_type=jnp.float32
    )
    return (first_grad, second_grad, keys_grad, values_grad)


def build_tokens(words, entities, positions, full_position):
    nearby = full_position[positions]
    tokens = jnp.concatenate(
        [words.astype(jnp.float32), entities.astype(jnp.float32) + nearby.astype(jnp.float32)],
        axis=1,
    )
    return (tokens, tokens.astype(jnp.bfloat16))


def tail_forward(resid_one, layer):
    gain_one, bias_one, full_up, full_down, gain_two, bias_two = layer
    hidden_one, normal_one, inverse_one = norm_forward(resid_one, gain_one, bias_one)
    hidden_low = hidden_one.astype(jnp.bfloat16)
    up = matmul(hidden_low, full_up)
    act_low = (0.5 * up * (1.0 + lax.erf(up * HALF_ROOT))).astype(jnp.bfloat16)
    hidden_two, normal_two, inverse_two = norm_forward(
        hidden_one + matmul(act_low, full_down), gain_two, bias_two
    )
    return (hidden_two, (normal_one, inverse_one, hidden_low, up, act_low, normal_two, inverse_two))


def tail_backward(hidden_grad, saved, layer, need_weights):
    gain_one, bias_one, full_up, full_down, gain_two, bias_two = layer
    normal_one, inverse_one, hidden_low, up, act_low, normal_two, inverse_two = saved
    resid_two_grad, gain_two_grad, bias_two_grad = norm_backward(
        hidden_grad, normal_two, inverse_two, gain_two
    )
    ffn_low = resid_two_grad.astype(jnp.bfloat16)
    act_grad = matmul_back(ffn_low, full_down)
    slope = 0.5 * (1.0 + lax.erf(up * HALF_ROOT)) + up * jnp.exp(-0.5 * up * up) * NORMAL_PEAK
    up_low = (act_grad * slope).astype(jnp.bfloat16)
    hidden_one_grad = resid_two_grad + matmul_back(up_low, full_up)
    resid_one_grad, gain_one_grad, bias_one_grad = norm_backward(
        hidden_one_grad, normal_one, inverse_one, gain_one
    )
    if not need_weights:
        return (resid_one_grad, ())
    down_grad = weight_grad(act_low, ffn_low)
    up_grad = weight_grad(hidden_low, up_low)
    return (
        resid_one_grad,
        (gain_one_grad, bias_one_grad, up_grad, down_grad, gain_two_grad, bias_two_grad),
    )


def entity_map(hidden_entities, slots, full_dense):
    picked = gather_rows(hidden_entities, jnp.maximum(slots, 0)).astype(jnp.bfloat16)
    mapped = jnp.einsum(
        "rsd,de->rse", picked, full_dense, preferred_element_type=jnp.float32
    ).astype(jnp.bfloat16)
    return (picked, mapped)


def entity_back(mapped_grad, picked, slots, full_dense, length, need_dense):
    picked_grad = jnp.einsum(
        "rse,de->rsd", mapped_grad, full_dense, preferred_element_type=jnp.float32
    )
    rows_grad = spread_rows(picked_grad, jnp.maximum(slots, 0), length)
    if not need_dense:
        return (rows_grad, None)
    return (
        rows_grad,
        jnp.einsum("rsd,rse->de", picked, mapped_grad, preferred_element_type=jnp.float32),
    )


def vocab_part(rows, tags, table, ids):
    logits = jnp.einsum("gd,vd->gv", rows, table, preferred_element_type=jnp.float32)
    top = jnp.max(logits, axis=-1)
    total = jnp.sum(jnp.exp(logits - top[:, None]), axis=-1)
    label = jnp.sum(jnp.where(tags[:, None] == ids[None, :], logits, 0.0), axis=-1)
    return (logits, top + jnp.log(total), label)


def vocab_grad(logits, tags, ids, norms, scales):
    hits = (tags[:, None] == ids[None, :]).astype(jnp.float32)
    return ((jnp.exp(logits - norms[:, None]) - hits) * scales[:, None]).astype(jnp.bfloat16)


def norm_rows(vectors):
    columns = jnp.stack(vectors, axis=1)
    return jnp.pad(columns, ((0, 0), (0, max(lax.axis_size("narrow") - len(vectors), 0))))


def tagged(slots, labels):
    return jnp.where(slots >= 0, labels, -1).reshape(-1)


def body(
    words_first,
    entities_first,
    positions_first,
    entity_slots_first,
    entity_labels_first,
    words_second,
    entities_second,
    positions_second,
    word_slots_second,
    word_labels_second,
    entity_slots_second,
    entity_labels_second,
    query_word_word,
    query_word_entity,
    query_entity_word,
    query_entity_entity,
    key_weight,
    value_weight,
    output_weight,
    attention_gain,
    attention_bias,
    up_weight,
    down_weight,
    feedforward_gain,
    feedforward_bias,
    word_table,
    entity_dense,
    entity_table,
    position_table,
):
    row_count = words_second.shape[0]
    split = words_second.shape[1]
    width = words_second.shape[2]
    ent_count = entities_second.shape[1]
    length = split + ent_count
    (
        full_position,
        full_ew,
        full_ee,
        full_key,
        full_value,
        full_ww,
        full_we,
        gain_one,
        bias_one,
        gain_two,
        bias_two,
    ) = gather_weights(
        (
            position_table,
            query_entity_word,
            query_entity_entity,
            key_weight,
            value_weight,
            query_word_word,
            query_word_entity,
            attention_gain,
            attention_bias,
            feedforward_gain,
            feedforward_bias,
        )
    )
    full_output, full_up, full_down, full_dense = gather_weights(
        (output_weight, up_weight, down_weight, entity_dense)
    )
    layer = (gain_one, bias_one, full_up, full_down, gain_two, bias_two)
    ent_width = full_dense.shape[1]
    tokens_one, low_one = build_tokens(words_first, entities_first, positions_first, full_position)
    entity_one = low_one[:, split:]
    keys_one = to_groups(
        matmul(low_one, full_key).astype(jnp.bfloat16).reshape(row_count, length, HEADS, HD)
    )
    values_one = to_groups(
        matmul(low_one, full_value).astype(jnp.bfloat16).reshape(row_count, length, HEADS, HD)
    )
    first_one = to_groups(
        matmul(entity_one, full_ew).astype(jnp.bfloat16).reshape(row_count, ent_count, HEADS, HD)
    )
    second_one = to_groups(
        matmul(entity_one, full_ee).astype(jnp.bfloat16).reshape(row_count, ent_count, HEADS, HD)
    )
    context_one, lse_one = lax.map(
        lambda part: attention_forward(part[0], part[1], part[2], part[3], split),
        (first_one, second_one, keys_one, values_one),
    )
    context_one_low = from_groups(context_one, row_count)
    hidden_one, saved_one = tail_forward(
        tokens_one[:, split:] + matmul(context_one_low, full_output), layer
    )
    picked_one, mapped_one = entity_map(hidden_one, entity_slots_first, full_dense)
    tokens_two, low_two = build_tokens(
        words_second, entities_second, positions_second, full_position
    )
    word_low = low_two[:, :split]
    entity_low = low_two[:, split:]
    first_two = to_groups(
        jnp.concatenate([matmul(word_low, full_ww), matmul(entity_low, full_ew)], axis=1)
        .astype(jnp.bfloat16)
        .reshape(row_count, length, HEADS, HD)
    )
    second_two = to_groups(
        jnp.concatenate([matmul(word_low, full_we), matmul(entity_low, full_ee)], axis=1)
        .astype(jnp.bfloat16)
        .reshape(row_count, length, HEADS, HD)
    )
    keys_two = to_groups(
        matmul(low_two, full_key).astype(jnp.bfloat16).reshape(row_count, length, HEADS, HD)
    )
    values_two = to_groups(
        matmul(low_two, full_value).astype(jnp.bfloat16).reshape(row_count, length, HEADS, HD)
    )
    context_two, lse_two = lax.map(
        lambda part: attention_forward(part[0], part[1], part[2], part[3], split),
        (first_two, second_two, keys_two, values_two),
    )
    context_low = from_groups(context_two, row_count)
    hidden_two, saved_two = tail_forward(tokens_two + matmul(context_low, full_output), layer)
    picked_two, mapped_two = entity_map(hidden_two[:, split:], entity_slots_second, full_dense)
    slot_count = word_slots_second.shape[1]
    ent_slots = entity_slots_second.shape[1]
    word_position = jnp.maximum(word_slots_second, 0)
    word_rows = (
        gather_rows(hidden_two[:, :split], word_position)
        .astype(jnp.bfloat16)
        .reshape(row_count * slot_count, width)
    )
    word_tags = tagged(word_slots_second, word_labels_second)
    tags_one = tagged(entity_slots_first, entity_labels_first)
    tags_two = tagged(entity_slots_second, entity_labels_second)
    words_held = row_count * slot_count
    ents_held = 2 * row_count * ent_slots
    ent_rows = ents_held * ent_width // WIDTH
    held = jnp.concatenate([mapped_one.reshape(-1, ent_width), mapped_two.reshape(-1, ent_width)])
    digits = as_digits(jnp.concatenate([word_tags, tags_one, tags_two])).reshape(-1)
    tag_rows = -(-digits.shape[0] // WIDTH)
    digits = jnp.pad(digits, (0, tag_rows * WIDTH - digits.shape[0])).reshape(tag_rows, WIDTH)
    sent = padded_rows(
        jnp.concatenate([word_rows, held.reshape(ent_rows, WIDTH), digits]), PAD
    )
    gathered = gather_relative(sent)
    devices = gathered.shape[0]
    row_stop = words_held + ent_rows
    all_words = gathered[:, :words_held].reshape(devices * words_held, width)
    all_held = gathered[:, words_held:row_stop].reshape(devices * ents_held, ent_width)
    all_digits = gathered[:, row_stop : row_stop + tag_rows].reshape(devices, tag_rows * WIDTH)
    tag_count = words_held + ents_held
    all_tags = from_digits(all_digits[:, : 3 * tag_count].reshape(devices, 3, tag_count))
    valid = (all_tags >= 0).astype(jnp.float32)
    half_held = words_held + ents_held // 2
    word_scale = 1.0 / jnp.sum(valid[:, :words_held])
    scale_one = 1.0 / jnp.sum(valid[:, words_held:half_held])
    scale_two = 1.0 / jnp.sum(valid[:, half_held:])
    column = jnp.arange(tag_count)[None, :]
    scales = valid * jnp.where(
        column < words_held, word_scale, jnp.where(column < half_held, scale_one, scale_two)
    )
    loss_scales = valid * jnp.where(
        column < words_held, word_scale, jnp.where(column < half_held, 0.0, scale_two)
    )
    me = lax.axis_index(("wide", "narrow"))
    word_shard = word_table.shape[0]
    ent_shard = entity_table.shape[0]
    word_ids = me * word_shard + jnp.arange(word_shard, dtype=jnp.int32)
    entity_ids = me * ent_shard + jnp.arange(ent_shard, dtype=jnp.int32)
    flat_word_tags = all_tags[:, :words_held].reshape(-1)
    flat_ent_tags = all_tags[:, words_held:].reshape(-1)
    word_logits, word_norms, word_label = vocab_part(
        all_words, flat_word_tags, word_table, word_ids
    )
    ent_logits, ent_norms, ent_label = vocab_part(
        all_held, flat_ent_tags, entity_table, entity_ids
    )
    norms = join_norms(
        jnp.concatenate(
            [word_norms.reshape(devices, words_held), ent_norms.reshape(devices, ents_held)], axis=1
        )
    )
    word_grad_low = vocab_grad(
        word_logits,
        flat_word_tags,
        word_ids,
        norms[:, :words_held].reshape(-1),
        scales[:, :words_held].reshape(-1),
    )
    ent_grad_low = vocab_grad(
        ent_logits,
        flat_ent_tags,
        entity_ids,
        norms[:, words_held:].reshape(-1),
        scales[:, words_held:].reshape(-1),
    )
    labels = jnp.concatenate(
        [word_label.reshape(devices, words_held), ent_label.reshape(devices, ents_held)], axis=1
    )
    loss_part = jnp.sum(norms[0] * loss_scales[0]) - jnp.sum(labels * loss_scales)
    partial_rows = jnp.einsum(
        "gv,vd->gd", word_grad_low, word_table, preferred_element_type=jnp.float32
    ).astype(jnp.bfloat16)
    partial_held = jnp.einsum(
        "gv,ve->ge", ent_grad_low, entity_table, preferred_element_type=jnp.float32
    ).astype(jnp.bfloat16)
    returned = scatter_relative(
        jnp.concatenate(
            [
                partial_rows.reshape(devices, words_held, WIDTH),
                partial_held.reshape(devices, ent_rows, WIDTH),
            ],
            axis=1,
        )
    )
    word_rows_grad = returned[:words_held].astype(jnp.float32)
    map_low = returned[words_held:].reshape(2, row_count, ent_slots, ent_width)
    map_low_one, map_low_two = map_low[0], map_low[1]
    table_grad = jnp.einsum(
        "gv,gd->vd", word_grad_low, all_words, preferred_element_type=jnp.float32
    )
    second_held = jnp.where(
        jnp.arange(ents_held)[None, :, None] >= ents_held // 2,
        all_held.reshape(devices, ents_held, ent_width),
        jnp.zeros((), jnp.bfloat16),
    ).reshape(-1, ent_width)
    etable_grad = jnp.einsum(
        "gv,ge->ve", ent_grad_low, second_held, preferred_element_type=jnp.float32
    )
    loss_second = loss_part
    for axis, mask in mesh_stages():
        loss_second = loss_second + exchange(loss_second, axis, mask)
    entity_grad_one = entity_back(
        map_low_one, picked_one, entity_slots_first, full_dense, ent_count, False
    )[0]
    resid_one_grad = tail_backward(entity_grad_one, saved_one, layer, False)[0]
    context_one_grad = to_groups(
        matmul_back(resid_one_grad.astype(jnp.bfloat16), full_output)
        .astype(jnp.bfloat16)
        .reshape(row_count, ent_count, HEADS, HD)
    )
    first_one_grad, second_one_grad = lax.map(
        lambda part: attention_backward(
            part[0], part[1], part[2], part[3], part[4], part[5], split, False
        ),
        (first_one, second_one, keys_one, values_one, lse_one, context_one_grad),
    )
    ew_first = weight_grad(entity_one, from_groups(first_one_grad, row_count).astype(jnp.bfloat16))
    ee_first = weight_grad(entity_one, from_groups(second_one_grad, row_count).astype(jnp.bfloat16))
    entity_rows_grad, dense_grad = entity_back(
        map_low_two, picked_two, entity_slots_second, full_dense, ent_count, True
    )
    word_spread = spread_rows(
        word_rows_grad.reshape(row_count, slot_count, width), word_position, split
    )
    hidden_grad = jnp.concatenate([word_spread, entity_rows_grad], axis=1)
    resid_grad, tail_grads = tail_backward(hidden_grad, saved_two, layer, True)
    gain_one_grad, bias_one_grad, up_grad, down_grad, gain_two_grad, bias_two_grad = tail_grads
    attended_low = resid_grad.astype(jnp.bfloat16)
    output_grad = weight_grad(context_low, attended_low)
    context_grad = to_groups(
        matmul_back(attended_low, full_output)
        .astype(jnp.bfloat16)
        .reshape(row_count, length, HEADS, HD)
    )
    first_grad, second_grad, keys_grad, values_grad = lax.map(
        lambda part: attention_backward(
            part[0], part[1], part[2], part[3], part[4], part[5], split, True
        ),
        (first_two, second_two, keys_two, values_two, lse_two, context_grad),
    )
    first_low = from_groups(first_grad, row_count).astype(jnp.bfloat16)
    second_low = from_groups(second_grad, row_count).astype(jnp.bfloat16)
    keys_low = from_groups(keys_grad, row_count).astype(jnp.bfloat16)
    values_low = from_groups(values_grad, row_count).astype(jnp.bfloat16)
    grad_ww = weight_grad(word_low, first_low[:, :split])
    grad_ew = weight_grad(entity_low, first_low[:, split:])
    grad_we = weight_grad(word_low, second_low[:, :split])
    grad_ee = weight_grad(entity_low, second_low[:, split:])
    grad_key = weight_grad(low_two, keys_low)
    grad_value = weight_grad(low_two, values_low)
    query_back = jnp.concatenate(
        [
            matmul_back(first_low[:, :split], full_ww)
            + matmul_back(second_low[:, :split], full_we),
            matmul_back(first_low[:, split:], full_ew)
            + matmul_back(second_low[:, split:], full_ee),
        ],
        axis=1,
    )
    tokens_grad = (
        resid_grad
        + matmul_back(keys_low, full_key)
        + matmul_back(values_low, full_value)
        + query_back
    )
    entity_tokens_grad = tokens_grad[:, split:]
    words_grad = tokens_grad[:, :split].astype(jnp.bfloat16)
    entities_grad = entity_tokens_grad.astype(jnp.bfloat16)
    position_grad = jnp.sum(spread_rows(entity_tokens_grad, positions_second, split), axis=0)
    down_sum, up_sum = reduce_grads((down_grad, up_grad))
    output_sum, dense_sum, ew_first_sum, ee_first_sum, norm_sum = reduce_grads(
        (
            output_grad,
            dense_grad,
            ew_first,
            ee_first,
            norm_rows((gain_one_grad, bias_one_grad, gain_two_grad, bias_two_grad)),
        )
    )
    ww_sum, we_sum, key_sum = reduce_grads((grad_ww, grad_we, grad_key))
    ew_sum, ee_sum, value_sum, position_sum = reduce_grads(
        (grad_ew, grad_ee, grad_value, position_grad)
    )
    return (
        ew_first_sum,
        ee_first_sum,
        loss_second,
        words_grad,
        entities_grad,
        ww_sum,
        we_sum,
        ew_sum,
        ee_sum,
        key_sum,
        value_sum,
        output_sum,
        norm_sum[:, 0],
        norm_sum[:, 1],
        up_sum,
        down_sum,
        norm_sum[:, 2],
        norm_sum[:, 3],
        table_grad,
        dense_sum,
        etable_grad,
        position_sum,
    )


def solution(mesh):
    placed = (
        P(("wide", "narrow"), None, None),
        P(("wide", "narrow"), None, None),
        P(("wide", "narrow"), None),
        P(("wide", "narrow"), None),
        P(("wide", "narrow"), None),
        P(("wide", "narrow"), None, None),
        P(("wide", "narrow"), None, None),
        P(("wide", "narrow"), None),
        P(("wide", "narrow"), None),
        P(("wide", "narrow"), None),
        P(("wide", "narrow"), None),
        P(("wide", "narrow"), None),
        P("narrow", None),
        P("narrow", None),
        P("narrow", None),
        P("narrow", None),
        P("narrow", None),
        P("narrow", None),
        P("narrow", None),
        P("narrow"),
        P("narrow"),
        P("narrow", None),
        P("narrow", None),
        P("narrow"),
        P("narrow"),
        P(("wide", "narrow"), None),
        P("narrow", None),
        P(("wide", "narrow"), None),
        P("narrow", None),
    )
    return jax.shard_map(
        body,
        mesh=mesh,
        in_specs=placed,
        out_specs=(
            P("narrow", None),
            P("narrow", None),
            P(),
            P(("wide", "narrow"), None, None),
            P(("wide", "narrow"), None, None),
            P("narrow", None),
            P("narrow", None),
            P("narrow", None),
            P("narrow", None),
            P("narrow", None),
            P("narrow", None),
            P("narrow", None),
            P("narrow"),
            P("narrow"),
            P("narrow", None),
            P("narrow", None),
            P("narrow"),
            P("narrow"),
            P(("wide", "narrow"), None),
            P("narrow", None),
            P(("wide", "narrow"), None),
            P("narrow", None),
        ),
        check_vma=False,
    )
```

```python
import jax
import jax.numpy as jnp
from jax import lax
from jax.sharding import PartitionSpec as P

HEADS = 12
HD = 64


EPS = 1e-05
HALF_ROOT = 0.7071067811865476
NORMAL_PEAK = 0.3989422804014327

WIDTH = 768
LANES = 128


def bits_of(axis):
    size = lax.axis_size(axis)
    masks = []
    mask = 1
    while mask < size:
        masks.append(mask)
        mask *= 2
    return masks


def exchange(value, axis, mask):
    size = lax.axis_size(axis)
    return lax.ppermute(value, axis, [(place, place ^ mask) for place in range(size)])


def joined_low(mine, theirs):
    return (mine.astype(jnp.float32) + theirs.astype(jnp.float32)).astype(jnp.bfloat16)


def narrow_stages():
    return [("narrow", mask) for mask in bits_of("narrow")]


def wide_stages():
    return [("wide", mask) for mask in bits_of("wide")]


def scatter_stages():
    narrow, wide = narrow_stages(), wide_stages()
    return narrow[:1] + wide[1:2] + wide[:1] + narrow[1:] + wide[2:]


def gather_stages():
    return scatter_stages()[::-1]


def relative_ids():
    ids = [0]
    for axis, mask in gather_stages():
        step = mask * (lax.axis_size("narrow") if axis == "wide" else 1)
        ids = ids + [one ^ step for one in ids]
    return ids


def gather_relative(block):
    value = block[None]
    for axis, mask in gather_stages():
        value = jnp.concatenate([value, exchange(value, axis, mask)], axis=0)
    return value


def scatter_step(value, stage):
    half = value.shape[0] // 2
    return joined_low(value[:half], exchange(value[half:], *stage))


def sum_all(value, stages):
    for axis, mask in stages:
        value = value + exchange(value, axis, mask)
    return value


def meet(value, *others):
    return lax.optimization_barrier((value,) + others)


class Flow:

    def __init__(self, value, steps):
        self.value = value
        self.steps = list(steps)
        self.step()

    def step(self):
        if self.steps:
            self.value = self.steps.pop(0)(self.value)

    def finish(self):
        while self.steps:
            self.step()
        return self.value


def advance(value, flows, *others):
    held = meet(value, *(flow.value for flow in flows), *others)
    for flow, arrived in zip(flows, held[1:]):
        flow.value = arrived
        flow.step()
    return held[0]


def gather_steps():
    return [
        lambda value, stage=stage: jnp.concatenate([value, exchange(value, *stage)], axis=0)
        for stage in gather_stages()
    ]


def scatter_steps():
    return [lambda value, stage=stage: scatter_step(value, stage) for stage in scatter_stages()]


def sum_steps():
    stages = narrow_stages() + wide_stages()
    return [lambda value, stage=stage: value + exchange(value, *stage) for stage in stages]


def side_of(axis, mask):
    return (lax.axis_index(axis) // mask) % 2


def halves(value, dim, side):
    mine = lax.dynamic_index_in_dim(value, side, dim, keepdims=False)
    theirs = lax.dynamic_index_in_dim(value, 1 - side, dim, keepdims=False)
    return (mine, theirs)


class Chunk:

    def __init__(self, parts, stages):
        self.rows = [part.shape[1] for part in parts]
        self.parts = parts
        self.value = None
        wide = [stage for stage in stages if stage[0] == "wide"]
        self.left = [(stage, True) for stage in stages] + [(stage, False) for stage in wide[::-1]]
        self.step()

    def step(self):
        if not self.left:
            return
        (axis, mask), reduces = self.left.pop(0)
        side = side_of(axis, mask)
        if not reduces:
            theirs = exchange(self.value, axis, mask)
            self.value = jnp.where(
                side == 0,
                jnp.concatenate([self.value, theirs], axis=1),
                jnp.concatenate([theirs, self.value], axis=1),
            )
            return
        pairs = [self.split(part, axis, side) for part in self.parts or [self.value]]
        self.parts = None
        mine = jnp.concatenate([pair[0] for pair in pairs], axis=1)
        theirs = jnp.concatenate([pair[1] for pair in pairs], axis=1)
        self.value = joined_low(mine, exchange(theirs, axis, mask))

    def split(self, part, axis, side):
        count, rows, columns = part.shape
        if axis == "narrow":
            return halves(part.reshape(count // 2, 2, rows, columns), 1, side)
        return halves(part.reshape(count, 2, rows // 2, columns), 1, side)

    def finish(self):
        while self.left:
            self.step()
        total = self.value[0]
        shards = []
        start = 0
        for rows in self.rows:
            shards.append(total[start : start + rows].astype(jnp.float32))
            start += rows
        return shards


def blocks_of(grad):
    count = lax.axis_size("narrow")
    return grad.astype(jnp.bfloat16).reshape(count, grad.shape[0] // count, grad.shape[1])


def gather_norms(vectors):
    count = lax.axis_size("narrow")
    own = jnp.stack(vectors)
    placed = jnp.where(
        jnp.arange(count)[:, None, None] == lax.axis_index("narrow"), own[None], jnp.zeros_like(own)
    )
    placed = sum_all(placed, narrow_stages())
    whole = jnp.transpose(placed, (1, 0, 2)).reshape(len(vectors), -1)
    return [whole[place] for place in range(len(vectors))]


def matmul(inputs, weight):
    return jnp.einsum("rld,de->rle", inputs, weight, preferred_element_type=jnp.float32)


def matmul_back(grads, weight):
    return jnp.einsum("rle,de->rld", grads, weight, preferred_element_type=jnp.float32)


def weight_grad(inputs, grads):
    return jnp.einsum("rld,rle->de", inputs, grads, preferred_element_type=jnp.float32)


def gather_rows(values, position):
    return jax.vmap(lambda table, picked: table[picked])(values, position)


def spread_rows(grads, position, length):
    onehot = (position[:, :, None] == jnp.arange(length)[None, None, :]).astype(jnp.float32)
    return jnp.einsum("rsn,rsd->rnd", onehot, grads, precision=lax.Precision.HIGHEST)


def head_groups():
    return 2


def to_groups(values):
    rows, count = (values.shape[0], values.shape[1])
    groups = head_groups()
    shaped = values.reshape(rows, count, groups, HEADS // groups, HD)
    return jnp.transpose(shaped, (0, 2, 1, 3, 4)).reshape(rows * groups, count, HEADS // groups, HD)


def from_groups(values, rows):
    groups = head_groups()
    count = values.shape[1]
    shaped = values.reshape(rows, groups, count, HEADS // groups, HD)
    return jnp.transpose(shaped, (0, 2, 1, 3, 4)).reshape(rows, count, HEADS * HD)


def norm_forward(resid, gain, bias):
    average = jnp.mean(resid, axis=-1, keepdims=True)
    centered = resid - average
    inverse = lax.rsqrt(jnp.mean(centered * centered, axis=-1, keepdims=True) + EPS)
    normal = centered * inverse
    return (normal * gain.astype(jnp.float32) + bias.astype(jnp.float32), normal, inverse)


def norm_backward(grads, normal, inverse, gain):
    scaled = grads * gain.astype(jnp.float32)
    centered = scaled - jnp.mean(scaled, axis=-1, keepdims=True)
    resid_grad = inverse * (centered - normal * jnp.mean(scaled * normal, axis=-1, keepdims=True))
    return (resid_grad, jnp.sum(grads * normal, axis=(0, 1)), jnp.sum(grads, axis=(0, 1)))


def score_block(first, second, keys, split):
    scores = jnp.concatenate(
        [
            jnp.einsum("qhd,khd->hqk", first, keys[:split], preferred_element_type=jnp.float32),
            jnp.einsum("qhd,khd->hqk", second, keys[split:], preferred_element_type=jnp.float32),
        ],
        axis=-1,
    )
    return scores * HD ** (-0.5)


def attention_forward(first, second, keys, values, split):
    scores = score_block(first, second, keys, split)
    top = jnp.max(scores, axis=-1, keepdims=True)
    expo = jnp.exp(scores - top)
    total = jnp.sum(expo, axis=-1, keepdims=True)
    probs_low = (expo / total).astype(jnp.bfloat16)
    context = jnp.einsum("hqk,khd->qhd", probs_low, values, preferred_element_type=jnp.float32)
    return (context.astype(jnp.bfloat16), (top + jnp.log(total))[..., 0])


def attention_backward(first, second, keys, values, lse, context_grad, split, with_keys):
    scale = HD ** (-0.5)
    scores = score_block(first, second, keys, split)
    probs = jnp.exp(scores - lse[..., None])
    probs_grad = jnp.einsum(
        "qhd,khd->hqk", context_grad, values, preferred_element_type=jnp.float32
    )
    scores_grad = (
        probs * (probs_grad - jnp.sum(probs * probs_grad, axis=-1, keepdims=True))
    ).astype(jnp.bfloat16)
    first_grad = (
        jnp.einsum(
            "hqk,khd->qhd",
            scores_grad[..., :split],
            keys[:split],
            preferred_element_type=jnp.float32,
        )
        * scale
    )
    second_grad = (
        jnp.einsum(
            "hqk,khd->qhd",
            scores_grad[..., split:],
            keys[split:],
            preferred_element_type=jnp.float32,
        )
        * scale
    )
    if not with_keys:
        return (first_grad, second_grad)
    keys_grad = (
        jnp.concatenate(
            [
                jnp.einsum(
                    "hqk,qhd->khd",
                    scores_grad[..., :split],
                    first,
                    preferred_element_type=jnp.float32,
                ),
                jnp.einsum(
                    "hqk,qhd->khd",
                    scores_grad[..., split:],
                    second,
                    preferred_element_type=jnp.float32,
                ),
            ],
            axis=0,
        )
        * scale
    )
    values_grad = jnp.einsum(
        "hqk,qhd->khd", probs.astype(jnp.bfloat16), context_grad, preferred_element_type=jnp.float32
    )
    return (first_grad, second_grad, keys_grad, values_grad)


def build_tokens(words, entities, positions, full_position):
    nearby = full_position[positions]
    tokens = jnp.concatenate(
        [words.astype(jnp.float32), entities.astype(jnp.float32) + nearby.astype(jnp.float32)],
        axis=1,
    )
    return (tokens, tokens.astype(jnp.bfloat16))


def tail_forward(resid_one, layer):
    gain_one, bias_one, full_up, full_down, gain_two, bias_two = layer
    hidden_one, normal_one, inverse_one = norm_forward(resid_one, gain_one, bias_one)
    hidden_low = hidden_one.astype(jnp.bfloat16)
    up = matmul(hidden_low, full_up)
    act_low = (0.5 * up * (1.0 + lax.erf(up * HALF_ROOT))).astype(jnp.bfloat16)
    hidden_two, normal_two, inverse_two = norm_forward(
        hidden_one + matmul(act_low, full_down), gain_two, bias_two
    )
    return (hidden_two, (normal_one, inverse_one, hidden_low, up, act_low, normal_two, inverse_two))


def tail_backward(hidden_grad, saved, layer, need_weights):
    gain_one, bias_one, full_up, full_down, gain_two, bias_two = layer
    normal_one, inverse_one, hidden_low, up, act_low, normal_two, inverse_two = saved
    resid_two_grad, gain_two_grad, bias_two_grad = norm_backward(
        hidden_grad, normal_two, inverse_two, gain_two
    )
    ffn_low = resid_two_grad.astype(jnp.bfloat16)
    act_grad = matmul_back(ffn_low, full_down)
    slope = 0.5 * (1.0 + lax.erf(up * HALF_ROOT)) + up * jnp.exp(-0.5 * up * up) * NORMAL_PEAK
    up_low = (act_grad * slope).astype(jnp.bfloat16)
    hidden_one_grad = resid_two_grad + matmul_back(up_low, full_up)
    resid_one_grad, gain_one_grad, bias_one_grad = norm_backward(
        hidden_one_grad, normal_one, inverse_one, gain_one
    )
    if not need_weights:
        return (resid_one_grad, ())
    down_grad = weight_grad(act_low, ffn_low)
    up_grad = weight_grad(hidden_low, up_low)
    return (
        resid_one_grad,
        (gain_one_grad, bias_one_grad, up_grad, down_grad, gain_two_grad, bias_two_grad),
    )


def entity_map(hidden_entities, slots, full_dense):
    picked = gather_rows(hidden_entities, jnp.maximum(slots, 0)).astype(jnp.bfloat16)
    mapped = jnp.einsum(
        "rsd,de->rse", picked, full_dense, preferred_element_type=jnp.float32
    ).astype(jnp.bfloat16)
    return (picked, mapped)


def entity_back(mapped_grad, picked, slots, full_dense, length, need_dense):
    picked_grad = jnp.einsum(
        "rse,de->rsd", mapped_grad, full_dense, preferred_element_type=jnp.float32
    )
    rows_grad = spread_rows(picked_grad, jnp.maximum(slots, 0), length)
    if not need_dense:
        return (rows_grad, None)
    return (
        rows_grad,
        jnp.einsum("rsd,rse->de", picked, mapped_grad, preferred_element_type=jnp.float32),
    )


def log_sum(logits):
    top = jnp.max(logits, axis=-1)
    return top + jnp.log(jnp.sum(jnp.exp(logits - top[:, None]), axis=-1))


def word_loss(rows, tags, scales, table, ids):
    logits = jnp.einsum("gd,vd->gv", rows, table, preferred_element_type=jnp.float32)
    norms = log_sum(logits)
    hits = tags[:, None] == ids[None, :]
    label = jnp.sum(jnp.where(hits, logits, 0.0), axis=-1)
    probs = jnp.exp(logits - norms[:, None])
    grad_low = ((probs - hits.astype(jnp.float32)) * scales[:, None]).astype(jnp.bfloat16)
    rows_grad = jnp.einsum("gv,vd->gd", grad_low, table, preferred_element_type=jnp.float32)
    table_grad = jnp.einsum("gv,gd->vd", grad_low, rows, preferred_element_type=jnp.float32)
    return (jnp.sum((norms - label) * scales), rows_grad, table_grad.astype(jnp.bfloat16))


def rounded(value):
    return lax.reduce_precision(value, 8, 7)


def as_parts(norms):
    high = rounded(norms)
    middle = rounded(norms - high)
    low = norms - high - middle
    lane = jnp.arange(LANES)
    parts = jnp.where(
        lane == 0, high, jnp.where(lane == 1, middle, jnp.where(lane == 2, low, 0.0))
    )
    return parts.astype(jnp.bfloat16)


def join_held(mine, theirs, width):
    mine, theirs = mine.astype(jnp.float32), theirs.astype(jnp.float32)
    norm = jnp.sum(mine[..., 2 * width :], axis=-1, keepdims=True)
    other = jnp.sum(theirs[..., 2 * width :], axis=-1, keepdims=True)
    top = jnp.maximum(norm, other)
    total = top + jnp.log(jnp.exp(norm - top) + jnp.exp(other - top))
    mean = mine[..., :width] * jnp.exp(norm - total) + theirs[..., :width] * jnp.exp(other - total)
    label = mine[..., width : 2 * width] + theirs[..., width : 2 * width]
    return jnp.concatenate(
        [mean.astype(jnp.bfloat16), label.astype(jnp.bfloat16), as_parts(total)], axis=-1
    )


def tagged(slots, labels):
    return jnp.where(slots >= 0, labels, -1).reshape(-1)


def body(
    words_first,
    entities_first,
    positions_first,
    entity_slots_first,
    entity_labels_first,
    words_second,
    entities_second,
    positions_second,
    word_slots_second,
    word_labels_second,
    entity_slots_second,
    entity_labels_second,
    query_word_word,
    query_word_entity,
    query_entity_word,
    query_entity_entity,
    key_weight,
    value_weight,
    output_weight,
    attention_gain,
    attention_bias,
    up_weight,
    down_weight,
    feedforward_gain,
    feedforward_bias,
    word_table,
    entity_dense,
    entity_table,
    position_table,
):
    row_count = words_second.shape[0]
    split = words_second.shape[1]
    width = words_second.shape[2]
    ent_count = entities_second.shape[1]
    length = split + ent_count
    mixed = jnp.concatenate([position_table, entity_dense.reshape(-1, width)], axis=0)
    gathered = lax.all_gather(
        jnp.stack(
            [
                mixed,
                key_weight,
                value_weight,
                query_entity_word,
                query_entity_entity,
                query_word_word,
                query_word_entity,
                output_weight,
            ]
        ),
        "narrow",
        axis=1,
        tiled=True,
    )
    full_key, full_value, full_ew, full_ee, full_ww, full_we, full_output = (
        gathered[place] for place in range(1, 8)
    )
    full_mixed = gathered[0].reshape(-1, mixed.shape[0], width)
    full_position = full_mixed[:, : position_table.shape[0]].reshape(-1, width)
    full_dense = full_mixed[:, position_table.shape[0] :].reshape(-1, entity_dense.shape[1])
    full_up = lax.all_gather(up_weight, "narrow", axis=0, tiled=True)
    full_down = lax.all_gather(down_weight, "narrow", axis=0, tiled=True)
    gain_one, bias_one, gain_two, bias_two = gather_norms(
        (attention_gain, attention_bias, feedforward_gain, feedforward_bias)
    )
    word_tags = tagged(word_slots_second, word_labels_second)
    tags_one = tagged(entity_slots_first, entity_labels_first)
    tags_two = tagged(entity_slots_second, entity_labels_second)
    own_tags = jnp.concatenate([tags_one, tags_two])
    held_count = own_tags.shape[0]
    own_count = jnp.sum(word_tags >= 0).astype(jnp.int32)
    noted = jnp.concatenate(
        [own_tags, own_count[None], jnp.full((-(held_count + 1) % LANES,), -1, jnp.int32)]
    )
    all_noted = gather_relative(noted)
    devices = all_noted.shape[0]
    all_tags = all_noted[:, :held_count]
    valid = (all_tags >= 0).astype(jnp.float32)
    half_held = held_count // 2
    word_scale = 1.0 / jnp.sum(all_noted[:, held_count]).astype(jnp.float32)
    scale_one = 1.0 / jnp.sum(valid[:, :half_held])
    scale_two = 1.0 / jnp.sum(valid[:, half_held:])
    table_flow = Flow(word_table[None], gather_steps())
    for _ in range(len(table_flow.steps) - 2):
        table_flow.step()
    word_shard = word_table.shape[0]
    ent_shard = entity_table.shape[0]
    me = lax.axis_index(("wide", "narrow"))
    owners = me ^ jnp.array(relative_ids(), dtype=jnp.int32)
    word_ids = (
        owners[:, None] * word_shard + jnp.arange(word_shard, dtype=jnp.int32)[None, :]
    ).reshape(-1)
    entity_ids = me * ent_shard + jnp.arange(ent_shard, dtype=jnp.int32)
    hits = all_tags.reshape(-1)[:, None] == entity_ids[None, :]
    label_rows = jnp.einsum(
        "gv,ve->ge",
        hits.astype(jnp.bfloat16),
        entity_table,
        preferred_element_type=jnp.float32,
    ).astype(jnp.bfloat16)
    layer = (gain_one, bias_one, full_up, full_down, gain_two, bias_two)
    ent_width = full_dense.shape[1]
    tokens_one, low_one = build_tokens(words_first, entities_first, positions_first, full_position)
    entity_one = low_one[:, split:]
    keys_one = to_groups(
        matmul(low_one, full_key).astype(jnp.bfloat16).reshape(row_count, length, HEADS, HD)
    )
    values_one = to_groups(
        matmul(low_one, full_value).astype(jnp.bfloat16).reshape(row_count, length, HEADS, HD)
    )
    first_one = to_groups(
        matmul(entity_one, full_ew).astype(jnp.bfloat16).reshape(row_count, ent_count, HEADS, HD)
    )
    second_one = to_groups(
        matmul(entity_one, full_ee).astype(jnp.bfloat16).reshape(row_count, ent_count, HEADS, HD)
    )
    context_one, lse_one = lax.map(
        lambda part: attention_forward(part[0], part[1], part[2], part[3], split),
        (first_one, second_one, keys_one, values_one),
    )
    tokens_two, low_two = build_tokens(
        words_second, entities_second, positions_second, full_position
    )
    low_two = advance(low_two, [table_flow])
    word_low = low_two[:, :split]
    entity_low = low_two[:, split:]
    first_two = to_groups(
        jnp.concatenate([matmul(word_low, full_ww), matmul(entity_low, full_ew)], axis=1)
        .astype(jnp.bfloat16)
        .reshape(row_count, length, HEADS, HD)
    )
    second_two = to_groups(
        jnp.concatenate([matmul(word_low, full_we), matmul(entity_low, full_ee)], axis=1)
        .astype(jnp.bfloat16)
        .reshape(row_count, length, HEADS, HD)
    )
    keys_two = to_groups(
        matmul(low_two, full_key).astype(jnp.bfloat16).reshape(row_count, length, HEADS, HD)
    )
    values_two = to_groups(
        matmul(low_two, full_value).astype(jnp.bfloat16).reshape(row_count, length, HEADS, HD)
    )
    context_two, lse_two = lax.map(
        lambda part: attention_forward(part[0], part[1], part[2], part[3], split),
        (first_two, second_two, keys_two, values_two),
    )
    context_low = advance(from_groups(context_two, row_count), [table_flow])
    context_one_low = from_groups(context_one, row_count)
    hidden_two, saved_two = tail_forward(tokens_two + matmul(context_low, full_output), layer)
    hidden_one, saved_one = tail_forward(
        tokens_one[:, split:] + matmul(context_one_low, full_output), layer
    )
    picked_one, mapped_one = entity_map(hidden_one, entity_slots_first, full_dense)
    picked_two, mapped_two = entity_map(hidden_two[:, split:], entity_slots_second, full_dense)
    slot_count = word_slots_second.shape[1]
    ent_slots = entity_slots_second.shape[1]
    word_position = jnp.maximum(word_slots_second, 0)
    word_rows = (
        gather_rows(hidden_two[:, :split], word_position)
        .astype(jnp.bfloat16)
        .reshape(row_count * slot_count, width)
    )
    own_held = jnp.concatenate(
        [mapped_one.reshape(-1, ent_width), mapped_two.reshape(-1, ent_width)]
    )
    held_flow = Flow(own_held[None], gather_steps())
    held_flow.step()
    word_rows = advance(word_rows, [held_flow])
    all_held = held_flow.finish().reshape(-1, ent_width)
    all_table = table_flow.finish()
    word_part, word_rows_grad, table_part = word_loss(
        word_rows,
        word_tags,
        (word_tags >= 0).astype(jnp.float32) * word_scale,
        all_table.reshape(-1, width),
        word_ids,
    )
    ent_logits = jnp.einsum("ge,ve->gv", all_held, entity_table, preferred_element_type=jnp.float32)
    ent_norms = log_sum(ent_logits)
    others = jnp.where(hits, 0.0, jnp.exp(ent_logits - ent_norms[:, None])).astype(jnp.bfloat16)
    means = jnp.einsum("gv,ve->ge", others, entity_table, preferred_element_type=jnp.float32)
    held = jnp.concatenate(
        [means.astype(jnp.bfloat16), label_rows, as_parts(ent_norms[:, None])], axis=-1
    ).reshape(devices, held_count, 2 * ent_width + LANES)
    for axis, mask in scatter_stages():
        half = held.shape[0] // 2
        held = join_held(held[:half], exchange(held[half:], axis, mask), ent_width)
    home = held[0].astype(jnp.float32)
    own_norm = jnp.sum(home[:, 2 * ent_width :], axis=-1)
    own_label = home[:, ent_width : 2 * ent_width]
    own_logit = jnp.sum(own_held.astype(jnp.float32) * own_label, axis=-1)
    own_valid = (own_tags >= 0).astype(jnp.float32)
    is_two = jnp.arange(held_count) >= half_held
    own_scale = own_valid * jnp.where(is_two, scale_two, scale_one)
    label_weight = jnp.exp(own_logit - own_norm) - 1.0
    map_low = (
        (home[:, :ent_width] + label_weight[:, None] * own_label) * own_scale[:, None]
    ).astype(jnp.bfloat16)
    map_low = map_low.reshape(2, row_count, ent_slots, ent_width)
    map_low_one, map_low_two = map_low[0], map_low[1]
    loss_part = word_part + jnp.sum(jnp.where(is_two, (own_norm - own_logit) * own_scale, 0.0))
    sum_flow = Flow(table_part.reshape(devices, word_shard, width), scatter_steps())
    norm_flow = Flow(own_norm[None], gather_steps())
    entity_rows_grad, dense_grad = entity_back(
        map_low_two, picked_two, entity_slots_second, full_dense, ent_count, True
    )
    word_spread = spread_rows(
        word_rows_grad.reshape(row_count, slot_count, width), word_position, split
    )
    hidden_grad = jnp.concatenate([word_spread, entity_rows_grad], axis=1)
    hidden_grad = advance(hidden_grad, [sum_flow, norm_flow])
    resid_grad, tail_grads = tail_backward(hidden_grad, saved_two, layer, True)
    gain_one_grad, bias_one_grad, up_grad, down_grad, gain_two_grad, bias_two_grad = tail_grads
    attended_low = resid_grad.astype(jnp.bfloat16)
    up_low = up_grad.astype(jnp.bfloat16)
    down_low = down_grad.astype(jnp.bfloat16)
    down_part = lax.psum_scatter(down_low, "narrow", scatter_dimension=0, tiled=True)
    up_part = lax.psum_scatter(up_low, "narrow", scatter_dimension=0, tiled=True)
    down_sum = lax.psum(down_part, "wide").astype(jnp.float32)
    up_sum = lax.psum(up_part, "wide").astype(jnp.float32)
    vectors = jnp.stack(
        [
            gain_one_grad,
            bias_one_grad,
            gain_two_grad,
            bias_two_grad,
            jnp.full((width,), loss_part),
        ]
    )
    entity_grad_one = entity_back(
        map_low_one, picked_one, entity_slots_first, full_dense, ent_count, False
    )[0]
    vector_flow = Flow(vectors, sum_steps())
    entity_grad_one = advance(entity_grad_one, [sum_flow, norm_flow], attended_low, up_low, down_low)
    resid_one_grad = tail_backward(entity_grad_one, saved_one, layer, False)[0]
    context_one_grad = to_groups(
        matmul_back(resid_one_grad.astype(jnp.bfloat16), full_output)
        .astype(jnp.bfloat16)
        .reshape(row_count, ent_count, HEADS, HD)
    )
    first_one_grad, second_one_grad = lax.map(
        lambda part: attention_backward(
            part[0], part[1], part[2], part[3], part[4], part[5], split, False
        ),
        (first_one, second_one, keys_one, values_one, lse_one, context_one_grad),
    )
    first_one_low = from_groups(first_one_grad, row_count).astype(jnp.bfloat16)
    second_one_low = from_groups(second_one_grad, row_count).astype(jnp.bfloat16)
    context_grad = to_groups(
        matmul_back(attended_low, full_output)
        .astype(jnp.bfloat16)
        .reshape(row_count, length, HEADS, HD)
    )
    narrow, wide = narrow_stages(), wide_stages()
    along_y = narrow + wide
    along_z = narrow[:1] + wide[1:2] + narrow[1:] + wide[:1] + wide[2:]
    groups = head_groups()
    flows = [sum_flow, norm_flow, vector_flow]
    chunks = []
    pieces = []
    ready = ()
    columns = width // groups
    for group in range(groups):
        parts = [
            held.reshape((row_count, groups) + held.shape[1:])[:, group]
            for held in (first_two, second_two, keys_two, values_two, lse_two, context_grad)
        ]
        if group == 0:
            ready = (first_one_low, second_one_low)
        parts[5] = advance(parts[5], flows, *ready)
        found = [
            attention_backward(*(part[row] for part in parts), split, True)
            for row in range(row_count)
        ]
        lows = [
            jnp.stack([one[place] for one in found])
            .astype(jnp.bfloat16)
            .reshape(row_count, length, columns)
            for place in range(4)
        ]
        pieces.append(lows)
        if group == groups - 1:
            lows[0] = advance(lows[0], flows + chunks)
        first_low, second_low, keys_low, values_low = lows
        grads = [
            weight_grad(word_low, first_low[:, :split]),
            weight_grad(word_low, second_low[:, :split]),
            weight_grad(low_two, keys_low),
            weight_grad(low_two, values_low),
            weight_grad(entity_low, first_low[:, split:]),
            weight_grad(entity_low, second_low[:, split:]),
        ]
        if group == 0:
            for start in range(0, width, columns):
                cut = slice(start, start + columns)
                grads.append(weight_grad(context_low, attended_low[..., cut]))
                grads.append(weight_grad(entity_one, first_one_low[..., cut]))
                grads.append(weight_grad(entity_one, second_one_low[..., cut]))
            grads.append(dense_grad.reshape(-1, columns))
        grads = [blocks_of(grad) for grad in grads]
        if group < groups - 1:
            chunks.append(Chunk(grads, along_z if group % 2 == 0 else along_y))
            ready = tuple(grads) + (down_part, up_part)
    first_low, second_low, keys_low, values_low = (
        jnp.concatenate([piece[place] for piece in pieces], axis=2) for place in range(4)
    )

    def tokens_back(rows, query_first, query_second):
        return (
            resid_grad[:, rows]
            + matmul_back(keys_low[:, rows], full_key)
            + matmul_back(values_low[:, rows], full_value)
            + matmul_back(first_low[:, rows], query_first)
            + matmul_back(second_low[:, rows], query_second)
        )

    entity_tokens_grad = tokens_back(slice(split, length), full_ew, full_ee)
    entities_grad = entity_tokens_grad.astype(jnp.bfloat16)
    position_grad = jnp.sum(spread_rows(entity_tokens_grad, positions_second, split), axis=0)
    for start in range(0, width, columns):
        grads.append(blocks_of(position_grad[:, start : start + columns]))
    chunks.append(Chunk(grads, along_y))
    words_grad = tokens_back(slice(0, split), full_ww, full_we).astype(jnp.bfloat16)
    finished = [chunk.finish() for chunk in chunks]
    ww_sum, we_sum, key_sum, value_sum, ew_sum, ee_sum = (
        jnp.concatenate([sums[place] for sums in finished], axis=1) for place in range(6)
    )
    output_sum, ew_first_sum, ee_first_sum = (
        jnp.concatenate([finished[0][6 + place + 3 * part] for part in range(groups)], axis=1)
        for place in range(3)
    )
    dense_sum = finished[0][-1].reshape(entity_dense.shape)
    position_sum = jnp.concatenate(finished[-1][6 : 6 + groups], axis=1)
    table_grad = sum_flow.finish()[0].astype(jnp.float32)
    vectors = vector_flow.finish()
    loss_second = vectors[4, 0]
    norm_count = attention_gain.shape[0]
    norm_sum = lax.dynamic_slice_in_dim(
        vectors, lax.axis_index("narrow") * norm_count, norm_count, 1
    )
    all_norms = norm_flow.finish()
    ent_scales = jnp.where(is_two, scale_two, 0.0)[None, :] * valid
    ent_grad_low = (
        (jnp.exp(ent_logits - all_norms.reshape(-1)[:, None]) - hits.astype(jnp.float32))
        * ent_scales.reshape(-1)[:, None]
    ).astype(jnp.bfloat16)
    etable_grad = jnp.einsum("gv,ge->ve", ent_grad_low, all_held, preferred_element_type=jnp.float32)
    return (
        ew_first_sum,
        ee_first_sum,
        loss_second,
        words_grad,
        entities_grad,
        ww_sum,
        we_sum,
        ew_sum,
        ee_sum,
        key_sum,
        value_sum,
        output_sum,
        norm_sum[0],
        norm_sum[1],
        up_sum,
        down_sum,
        norm_sum[2],
        norm_sum[3],
        table_grad,
        dense_sum,
        etable_grad,
        position_sum,
    )


def solution(mesh):
    placed = (
        P(("wide", "narrow"), None, None),
        P(("wide", "narrow"), None, None),
        P(("wide", "narrow"), None),
        P(("wide", "narrow"), None),
        P(("wide", "narrow"), None),
        P(("wide", "narrow"), None, None),
        P(("wide", "narrow"), None, None),
        P(("wide", "narrow"), None),
        P(("wide", "narrow"), None),
        P(("wide", "narrow"), None),
        P(("wide", "narrow"), None),
        P(("wide", "narrow"), None),
        P("narrow", None),
        P("narrow", None),
        P("narrow", None),
        P("narrow", None),
        P("narrow", None),
        P("narrow", None),
        P("narrow", None),
        P("narrow"),
        P("narrow"),
        P("narrow", None),
        P("narrow", None),
        P("narrow"),
        P("narrow"),
        P(("wide", "narrow"), None),
        P("narrow", None),
        P(("wide", "narrow"), None),
        P("narrow", None),
    )
    return jax.shard_map(
        body,
        mesh=mesh,
        in_specs=placed,
        out_specs=(
            P("narrow", None),
            P("narrow", None),
            P(),
            P(("wide", "narrow"), None, None),
            P(("wide", "narrow"), None, None),
            P("narrow", None),
            P("narrow", None),
            P("narrow", None),
            P("narrow", None),
            P("narrow", None),
            P("narrow", None),
            P("narrow", None),
            P("narrow"),
            P("narrow"),
            P("narrow", None),
            P("narrow", None),
            P("narrow"),
            P("narrow"),
            P(("wide", "narrow"), None),
            P("narrow", None),
            P(("wide", "narrow"), None),
            P("narrow", None),
        ),
        check_vma=False,
    )
```
